32 devices in a mesh: vel: 16 (over z, y, x), space: 2 (over core).
Axes of the slice: x: 2, y: 2, z: 4, core: 2. Of those that a mesh axis runs over, the one named last changes fastest.
Arguments:
- distribution: float32 [16384, 16, 128], P('vel', 'space'), may hold values from 0 to 11, as said below
- rate_class: int32 [16, 128], P('space'), may hold values from 0 to 7
- boundary_obstacle_indicator: int32 [16, 128], P('space'), may hold values 0 or 1
Outputs:
- field_out: float32 [16384, 16, 128], P('vel', 'space')
- latest_conserved_fields: float32 [5, 16, 128], P(None, 'space')
The draws below stay inside these ranges and needn't reach their ends.
Inputs may be any that keep to these rules, and one draw needn't show every extreme that they name: `distribution`: every entry positive.
All inputs are finite; a program needn't handle non-finite values. No bound on the sum of `boundary_obstacle_indicator` on one device may be relied on, other than what follows from the above.
Results may differ from the reference program's by a relative error of at most 0.0003.
Values sent between devices are 32-bit elements; how exact they have to be, the bound alone decides.
A program may use at most 64 MiB of HBM per device.

```python
import jax
import jax.numpy as jnp
from jax import lax

VX = 32
VY = 32
VZ = 16
GRID_COLS_SPAN = 128
ITERS = 2
SWEEPS = 4
NV = 16384
GRID_ROWS_SPAN = 16


def draw_distribution(key, part):
    stochastic_seeds = jax.random.split(jax.random.fold_in(key, 71), 6)
    index = jnp.arange(NV, dtype=jnp.int32)
    discrete_abscissa_xaxis = (-5.0 + ((index % VX).astype(jnp.float32) + 0.5) * (10.0 / VX))[:, None, None]
    discrete_abscissa_yaxis = (-5.0 + ((index // VX % VY).astype(jnp.float32) + 0.5) * (10.0 / VY))[:, None, None]
    discrete_abscissa_zaxis = (-5.0 + ((index // (VX * VY)).astype(jnp.float32) + 0.5) * (10.0 / VZ))[:, None, None]
    particle_concentration = jax.random.uniform(stochastic_seeds[0], (GRID_ROWS_SPAN, GRID_COLS_SPAN), jnp.float32, 0.5, 2.0)
    kinetic_thermal_level = jax.random.uniform(stochastic_seeds[1], (GRID_ROWS_SPAN, GRID_COLS_SPAN), jnp.float32, 0.6, 1.6)
    rough_macro_guess = 0.5
    flow_x = jax.random.uniform(stochastic_seeds[2], (GRID_ROWS_SPAN, GRID_COLS_SPAN), jnp.float32, -0.5, 0.5)
    flow_y = jax.random.uniform(stochastic_seeds[3], (GRID_ROWS_SPAN, GRID_COLS_SPAN), jnp.float32, -0.5, 0.5)
    flow_z = jax.random.uniform(stochastic_seeds[4], (GRID_ROWS_SPAN, GRID_COLS_SPAN), jnp.float32, -0.2, 0.2)
    noisy_disturbance = jax.random.uniform(stochastic_seeds[5], (NV, GRID_ROWS_SPAN, GRID_COLS_SPAN), jnp.float32, -1.0, 1.0)
    quadratic_deviation = (discrete_abscissa_xaxis - flow_x) ** 2 + (discrete_abscissa_yaxis - flow_y) ** 2 + (discrete_abscissa_zaxis - flow_z) ** 2
    integral_averages = particle_concentration * kinetic_thermal_level ** (-1.5) * jnp.exp(-0.5 * quadratic_deviation / kinetic_thermal_level) * (1.0 + rough_macro_guess * noisy_disturbance)
    return integral_averages.astype(jnp.float32)


def place_ends(result, own_key, least, top_value):
    place = [jax.random.randint(jax.random.fold_in(own_key, axis), (), 0, length) for axis, length in enumerate(result.shape)]
    widest = result.shape.index(max(result.shape))
    next_to = place[:widest] + [(place[widest] + 1) % result.shape[widest]] + place[widest + 1:]
    return result.at[tuple(place)].set(least).at[tuple(next_to)].set(top_value)


def setup_inputs(seed: int = 0) -> dict:
    keys = jax.random.split(jax.random.key(seed), 4)
    distribution = draw_distribution(jax.random.fold_in(keys[3], 71), 0)
    rate_class = place_ends(jax.random.randint(keys[1], (GRID_ROWS_SPAN, GRID_COLS_SPAN), 0, 8), jax.random.fold_in(keys[1], 1), 0, 7).astype(jnp.int32)
    boundary_obstacle_indicator = place_ends((jax.random.randint(keys[2], (GRID_ROWS_SPAN, GRID_COLS_SPAN), 0, 8) < 1).astype(jnp.int32), jax.random.fold_in(keys[2], 1), 0, 1)
    return {"distribution": distribution, "rate_class": rate_class, "boundary_obstacle_indicator": boundary_obstacle_indicator}


speed_edge = 5.0
marching_step_length = 0.1
momentum_thermal_ratio = 2.0 / 3.0
shear_power_law_index = 0.81
diffusivity = 1.0


def velocity_table(index):
    index_x = index % VX
    index_y = (index // VX) % VY
    index_z = index // (VX * VY)
    discrete_abscissa_xaxis = -speed_edge + (index_x.astype(jnp.float32) + 0.5) * (2.0 * speed_edge / VX)
    discrete_abscissa_yaxis = -speed_edge + (index_y.astype(jnp.float32) + 0.5) * (2.0 * speed_edge / VY)
    discrete_abscissa_zaxis = -speed_edge + (index_z.astype(jnp.float32) + 0.5) * (2.0 * speed_edge / VZ)
    return discrete_abscissa_xaxis, discrete_abscissa_yaxis, discrete_abscissa_zaxis


def moment_weights(discrete_abscissa_xaxis, discrete_abscissa_yaxis, discrete_abscissa_zaxis):
    square = discrete_abscissa_xaxis * discrete_abscissa_xaxis + discrete_abscissa_yaxis * discrete_abscissa_yaxis + discrete_abscissa_zaxis * discrete_abscissa_zaxis
    quadrature = (2.0 * speed_edge / VX) * (2.0 * speed_edge / VY) * (2.0 * speed_edge / VZ) / (2.0 * jnp.pi) ** 1.5
    rows = [jnp.ones_like(discrete_abscissa_xaxis), discrete_abscissa_xaxis, discrete_abscissa_yaxis, discrete_abscissa_zaxis, square, discrete_abscissa_xaxis * discrete_abscissa_xaxis, discrete_abscissa_yaxis * discrete_abscissa_yaxis,
            discrete_abscissa_xaxis * discrete_abscissa_yaxis, discrete_abscissa_xaxis * discrete_abscissa_zaxis, discrete_abscissa_yaxis * discrete_abscissa_zaxis, discrete_abscissa_xaxis * square, discrete_abscissa_yaxis * square, discrete_abscissa_zaxis * square]
    return jnp.stack(rows) * quadrature


def conserved(moments):
    return jnp.stack([moments[0], moments[1], moments[2], moments[3], 0.5 * moments[4]])


def heat_flux(moments):
    mass = moments[0]
    flow_x = moments[1] / mass
    flow_y = moments[2] / mass
    flow_z = moments[3] / mass
    p_xx = moments[5]
    p_yy = moments[6]
    p_zz = moments[4] - moments[5] - moments[6]
    p_xy = moments[7]
    p_xz = moments[8]
    p_yz = moments[9]
    flow_sq = flow_x * flow_x + flow_y * flow_y + flow_z * flow_z
    heat_x = 0.5 * (moments[10] - 2.0 * (flow_x * p_xx + flow_y * p_xy + flow_z * p_xz) - flow_x * moments[4] + 2.0 * mass * flow_sq * flow_x)
    heat_y = 0.5 * (moments[11] - 2.0 * (flow_x * p_xy + flow_y * p_yy + flow_z * p_yz) - flow_y * moments[4] + 2.0 * mass * flow_sq * flow_y)
    heat_z = 0.5 * (moments[12] - 2.0 * (flow_x * p_xz + flow_y * p_yz + flow_z * p_zz) - flow_z * moments[4] + 2.0 * mass * flow_sq * flow_z)
    return jnp.stack([heat_x, heat_y, heat_z])


def transport_block(field, discrete_abscissa_xaxis, discrete_abscissa_yaxis):
    courant_x = (marching_step_length * discrete_abscissa_xaxis)[:, None, None]
    courant_y = (marching_step_length * discrete_abscissa_yaxis)[:, None, None]
    from_left = jnp.roll(field, 1, 2)
    from_right = jnp.roll(field, -1, 2)
    term_y = jnp.where(courant_y > 0, courant_y * (field - from_left), courant_y * (from_right - field))
    from_above = jnp.roll(field, 1, 1)
    from_below = jnp.roll(field, -1, 1)
    term_x = jnp.where(courant_x > 0, courant_x * (field - from_above), courant_x * (from_below - field))
    return field - term_x - term_y


def collision_update_piece(convected_fields, discrete_abscissa_xaxis, discrete_abscissa_yaxis, discrete_abscissa_zaxis, particle_concentration, mean_drift_velocity, kinetic_thermal_level, energy_flux_components, collision_frequency, obstacle_indicators):
    diff_x = discrete_abscissa_xaxis - mean_drift_velocity[0]
    diff_y = discrete_abscissa_yaxis - mean_drift_velocity[1]
    diff_z = discrete_abscissa_zaxis - mean_drift_velocity[2]
    quadratic_deviation = diff_x * diff_x + diff_y * diff_y + diff_z * diff_z
    prefactor_amplitude = particle_concentration * kinetic_thermal_level ** (-1.5)
    local_gaussian_population = prefactor_amplitude * jnp.exp(-0.5 * quadratic_deviation / kinetic_thermal_level)
    skewed_correction_multiplier = (1.0 - momentum_thermal_ratio) / (5.0 * particle_concentration * kinetic_thermal_level * kinetic_thermal_level)
    projected_energy_flux = diff_x * energy_flux_components[0] + diff_y * energy_flux_components[1] + diff_z * energy_flux_components[2]
    goal_population = local_gaussian_population * (1.0 + skewed_correction_multiplier * projected_energy_flux * (quadratic_deviation / kinetic_thermal_level - 5.0))
    wall_state = particle_concentration * jnp.exp(-0.5 * (discrete_abscissa_xaxis * discrete_abscissa_xaxis + discrete_abscissa_yaxis * discrete_abscissa_yaxis + discrete_abscissa_zaxis * discrete_abscissa_zaxis))
    relaxed = convected_fields + collision_frequency * (goal_population - convected_fields)
    return jnp.where(obstacle_indicators > 0, wall_state, relaxed)


def diffuse(source):
    iterate = source
    for sweep_index in range(SWEEPS):
        beside = (jnp.roll(iterate, 1, 1) + jnp.roll(iterate, -1, 1)) + jnp.roll(iterate, 1, 2) + jnp.roll(iterate, -1, 2)
        iterate = (source + diffusivity * beside) / (1.0 + 4.0 * diffusivity)
    return iterate


def reference(distribution, rate_class, boundary_obstacle_indicator):
    index = jnp.arange(NV, dtype=jnp.int32)
    discrete_abscissa_xaxis, discrete_abscissa_yaxis, discrete_abscissa_zaxis = velocity_table(index)
    block_rows = VX * VY
    blocks_x = discrete_abscissa_xaxis.reshape(VZ, block_rows)
    blocks_y = discrete_abscissa_yaxis.reshape(VZ, block_rows)
    blocks_z = discrete_abscissa_zaxis.reshape(VZ, block_rows)
    reference_collision_freq = 0.5 * jnp.exp2(rate_class.astype(jnp.float32))
    field = distribution
    latest_conserved_fields = jnp.zeros((5, GRID_ROWS_SPAN, GRID_COLS_SPAN), jnp.float32)
    for step_index in range(ITERS):
        field_blocks = field.reshape(VZ, block_rows, GRID_ROWS_SPAN, GRID_COLS_SPAN)

        def move(items):
            return transport_block(items[0], items[1], items[2])

        convected_fields = lax.map(move, (field_blocks, blocks_x, blocks_y))

        def accumulate(total, items):
            weights = moment_weights(items[1], items[2], items[3])
            part_sum = jnp.dot(weights, items[0].reshape(block_rows, GRID_ROWS_SPAN * GRID_COLS_SPAN), precision=lax.Precision.HIGHEST, preferred_element_type=jnp.float32)
            return total + part_sum, None

        moments, unused = lax.scan(accumulate, jnp.zeros((13, GRID_ROWS_SPAN * GRID_COLS_SPAN), jnp.float32), (convected_fields, blocks_x, blocks_y, blocks_z))
        source = conserved(moments).reshape(5, GRID_ROWS_SPAN, GRID_COLS_SPAN)
        energy_flux_components = heat_flux(moments).reshape(3, GRID_ROWS_SPAN, GRID_COLS_SPAN)
        latest_conserved_fields = diffuse(source)
        particle_concentration = latest_conserved_fields[0]
        mean_drift_velocity = latest_conserved_fields[1:4] / particle_concentration
        kinetic_thermal_level = (2.0 * latest_conserved_fields[4] / particle_concentration - (mean_drift_velocity[0] * mean_drift_velocity[0] + mean_drift_velocity[1] * mean_drift_velocity[1] + mean_drift_velocity[2] * mean_drift_velocity[2])) / 3.0
        collision_frequency = 1.0 - jnp.exp(-marching_step_length * reference_collision_freq * particle_concentration * kinetic_thermal_level ** (1.0 - shear_power_law_index))

        def collide(items):
            return collision_update_piece(items[0], items[1][:, None, None], items[2][:, None, None], items[3][:, None, None],
                               particle_concentration, mean_drift_velocity, kinetic_thermal_level, energy_flux_components, collision_frequency, boundary_obstacle_indicator)

        field = lax.map(collide, (convected_fields, blocks_x, blocks_y, blocks_z)).reshape(NV, GRID_ROWS_SPAN, GRID_COLS_SPAN)
    return field, latest_conserved_fields
```

```python
import functools

import jax
import jax.numpy as jnp
from jax import lax
from jax.experimental import pallas as pl
from jax.experimental.pallas import tpu as pltpu
from jax.sharding import PartitionSpec as P

VX = 32
VY = 32
VZ = 16
HX = VX // 2
ITERS = 2
SWEEPS = 4
EDGE = 5.0
STEP = 0.1
PRANDTL = 2.0 / 3.0
SHEAR = 0.81
DIFFUSIVITY = 1.0
QUAD = (
    (2.0 * EDGE / VX) * (2.0 * EDGE / VY) * (2.0 * EDGE / VZ) / (2.0 * 3.141592653589793) ** 1.5
)
MESH = pl.DeviceIdType.MESH
f32 = jnp.float32


def speed_x(ix):
    return -EDGE + (ix + 0.5) * (2.0 * EDGE / VX)


def speed_y(iy):
    return -EDGE + (iy.astype(f32) + 0.5) * (2.0 * EDGE / VY)


def speed_z(iz):
    return -EDGE + (iz.astype(f32) + 0.5) * (2.0 * EDGE / VZ)


def velocity_base(vel_index, vel_count):
    first = vel_index * vel_count
    return lax.rem(lax.div(first, VX), VY), lax.div(first, VX * VY)


def diffuse_rows(rows_ref, tr_ref, row_count):
    total = row_count + 2 * SWEEPS
    src = [rows_ref[i] for i in range(total)]
    cols = src[0].shape[1]
    state = list(src)
    for sweep in range(SWEEPS):
        new = list(state)
        for i in range(sweep + 1, total - sweep - 1):
            beside = (
                state[i - 1]
                + state[i + 1]
                + pltpu.roll(state[i], 1, 1)
                + pltpu.roll(state[i], cols - 1, 1)
            )
            new[i] = (src[i] + DIFFUSIVITY * beside) * (1.0 / (1.0 + 4.0 * DIFFUSIVITY))
        state = new
    sub = lax.broadcasted_iota(jnp.int32, src[0].shape, 0)
    for r in range(row_count):
        tr_ref[r] = jnp.where(sub < 5, state[SWEEPS + r], src[SWEEPS + r])


def macro_tables(tr_ref, rate_ref, wall_ref, tab_x, tab_y, iy0, iz, iy_count):
    q = [tr_ref[:, k, :] for k in range(8)]
    density = q[0]
    inv_density = 1.0 / density
    ux, uy, uz = q[1] * inv_density, q[2] * inv_density, q[3] * inv_density
    temperature = (2.0 * q[4] * inv_density - (ux * ux + uy * uy + uz * uz)) / 3.0
    frequency = 0.5 * jnp.exp2(rate_ref[...].astype(f32))
    power = jnp.exp((1.0 - SHEAR) * jnp.log(temperature))
    rate = 1.0 - jnp.exp(-STEP * frequency * density * power)
    wall = wall_ref[...] > 0
    inv_t = 1.0 / temperature
    root = lax.rsqrt(temperature)
    prefactor = density * (root * root * root)
    coef = (1.0 - PRANDTL) / (5.0 * density * temperature * temperature)
    hx, hy, hz = coef * q[5], coef * q[6], coef * q[7]
    zero = jnp.zeros_like(density)
    sz = jnp.full(density.shape, speed_z(iz), f32)
    cz = sz - uz
    z2 = cz * cz * inv_t
    scale_z = rate * prefactor * jnp.exp(-0.5 * z2)
    wall_z = density * jnp.exp(-0.5 * sz * sz)
    qz = hz * cz

    def table_x(ix, carry):
        sx = jnp.full(density.shape, speed_x(ix.astype(f32)), f32)
        cx = sx - ux
        x2 = cx * cx * inv_t
        tab_x[0, ix] = jnp.exp(-0.5 * jnp.where(wall, sx * sx, x2))
        tab_x[1, ix] = jnp.where(wall, zero, hx * cx)
        tab_x[2, ix] = jnp.where(wall, zero, x2)
        return carry

    lax.fori_loop(0, VX, table_x, 0, unroll=4)

    def table_y(iy, carry):
        sy = jnp.full(density.shape, speed_y(iy0 + iy), f32)
        cy = sy - uy
        y2 = cy * cy * inv_t
        tab_y[0, iy] = jnp.where(wall, wall_z, scale_z) * jnp.exp(
            -0.5 * jnp.where(wall, sy * sy, y2)
        )
        tab_y[1, iy] = jnp.where(wall, zero, hy * cy + qz)
        tab_y[2, iy] = jnp.where(wall, zero, y2 + z2 - 5.0)
        return carry

    lax.fori_loop(0, iy_count, table_y, 0, unroll=min(4, iy_count))
    return jnp.where(wall, zero, 1.0 - rate)


def collide(load, store, tab_x, tab_y, keep, start, count):
    block = 4 if count % 4 == 0 else 2 if count % 2 == 0 else 1

    def body(step, carry):
        base = start + step * block
        g = [tab_y[0, base + b] for b in range(block)]
        h = [tab_y[1, base + b] for b in range(block)]
        r = [tab_y[2, base + b] for b in range(block)]
        for ix in range(VX):
            ex, ax, bx = tab_x[0, ix], tab_x[1, ix], tab_x[2, ix]
            for b in range(block):
                old = load(base + b, ix)
                shape = (ax + h[b]) * (bx + r[b]) + 1.0
                store(base + b, ix, keep * old + (ex * g[b]) * shape)
        return carry

    lax.fori_loop(0, count // block, body, 0)


def chunks_of(iy_count):
    return 4 if iy_count % 4 == 0 else 1


def heat_row(total, z1, z2, z3):
    def at(array, k):
        return array[k : k + 1, :]

    m0, m1, m2, m3 = at(total, 0), at(total, 1), at(total, 2), at(z1, 0)
    m5, m6, m7 = at(total, 3), at(total, 4), at(total, 5)
    m4 = m5 + m6 + at(z2, 0)
    m8, m9 = at(z1, 1), at(z1, 2)
    m10 = at(total, 6) + at(z2, 1)
    m11 = at(total, 7) + at(z2, 2)
    m12 = at(z1, 3) + at(z1, 4) + at(z3, 0)
    inv = 1.0 / m0
    ux, uy, uz = m1 * inv, m2 * inv, m3 * inv
    pzz = at(z2, 0)
    extra = 2.0 * m0 * (ux * ux + uy * uy + uz * uz) - m4
    heat_x = 0.5 * (m10 - 2.0 * (ux * m5 + uy * m7 + uz * m8) + extra * ux)
    heat_y = 0.5 * (m11 - 2.0 * (ux * m7 + uy * m6 + uz * m9) + extra * uy)
    heat_z = 0.5 * (m12 - 2.0 * (ux * m8 + uy * m9 + uz * pzz) + extra * uz)
    return [m0, m1, m2, m3, 0.5 * m4, heat_x, heat_y, heat_z]


def advance_kernel(
    groups,
    tiles,
    dist,
    rate_ref,
    wall_ref,
    conv_out,
    rows_out,
    pad,
    conv,
    hal_send,
    hal_recv,
    part,
    gath,
    row_send,
    rows,
    tr,
    tab_x,
    tab_y,
    in_sem,
    out_sem,
    hs_sem,
    hr_sem,
    rs_send,
    rs_recv,
    ag_send,
    ag_recv,
):
    iy_count, _, _, row_count, cols = dist.shape
    vel_count = iy_count * VX
    nch = chunks_of(iy_count)
    span = iy_count // nch
    me = lax.axis_index("vel")
    here = lax.axis_index("space")
    right = lax.rem(here + 1, tiles)
    left = lax.rem(here + tiles - 1, tiles)
    iy0, iz = velocity_base(me, vel_count)
    first_owner = groups // 2 - row_count // 2
    mine = me - first_owner
    owner = jnp.logical_and(mine >= 0, mine < row_count)

    def load_in(c, sign):
        lo = row_count * sign
        return pltpu.make_async_copy(
            dist.at[pl.ds(c * span, span), sign],
            pad.at[pl.ds(c * span, span), sign, :, pl.ds(lo, row_count), :],
            in_sem.at[c, sign],
        )

    for c in range(nch):
        for sign in range(2):
            load_in(c, sign).start()

    barrier = pltpu.get_barrier_semaphore()

    def greet(p, carry):
        @pl.when(p != me)
        def _():
            pl.semaphore_signal(
                barrier, inc=1, device_id={"vel": p, "space": here}, device_id_type=MESH
            )

        for other in (left, right):
            pl.semaphore_signal(
                barrier, inc=1, device_id={"vel": p, "space": other}, device_id_type=MESH
            )
        return carry

    lax.fori_loop(0, groups, greet, 0)
    pl.semaphore_wait(barrier, 3 * groups - 1)

    def halo(it, c, sign):
        return pltpu.make_async_remote_copy(
            src_ref=hal_send.at[it, sign, pl.ds(c * span, span)],
            dst_ref=hal_recv.at[it, sign, pl.ds(c * span, span)],
            send_sem=hs_sem.at[it, sign, c],
            recv_sem=hr_sem.at[it, sign, c],
            device_id={"vel": me, "space": right if sign else left},
            device_id_type=MESH,
        )

    def send_halo(it, c):
        def pack(j, carry):
            iy = c * span + j
            for sign in range(2):
                row = 2 * row_count - 1 if sign else 0
                for k in range(0, HX, 8):
                    hal_send[it, sign, iy, pl.ds(k, 8), :] = pad[iy, sign, pl.ds(k, 8), row, :]
            return carry

        lax.fori_loop(0, span, pack, 0)
        for sign in range(2):
            halo(it, c, sign).start()

    def take_halo(it, c):
        for sign in range(2):
            halo(it, c, sign).wait_recv()

        def unpack(j, carry):
            iy = c * span + j
            for sign in range(2):
                row = row_count - 1 if sign else row_count
                for k in range(0, HX, 8):
                    pad[iy, sign, pl.ds(k, 8), row, :] = hal_recv[it, sign, iy, pl.ds(k, 8), :]
            return carry

        lax.fori_loop(0, span, unpack, 0)

    def transport(c, sums):
        def body(j, sums):
            iy = c * span + j
            iyg = iy0 + iy
            sy = speed_y(iyg)
            cy = jnp.full((row_count, cols), STEP * jnp.abs(sy), f32)
            shift = jnp.where(iyg < VY // 2, cols - 1, 1).astype(jnp.int32)

            def moved(ix):
                sign, k = ix // HX, ix % HX
                lo = row_count * sign
                cur = pad[iy, sign, k, pl.ds(lo, row_count), :]
                near = pad[iy, sign, k, pl.ds(lo - 1 if sign else lo + 1, row_count), :]
                along = pltpu.roll(cur, shift, 1)
                cx = STEP * abs(speed_x(ix))
                new = cur + cx * (near - cur) + cy * (along - cur)
                conv[iy * VX + ix] = new
                return new

            s0 = s1 = s2 = s3 = jnp.zeros((row_count, cols), f32)
            for k in range(HX):
                low, high = moved(k), moved(VX - 1 - k)
                sx = speed_x(VX - 1 - k)
                even, odd = high + low, sx * (high - low)
                s0 = s0 + even
                s1 = s1 + odd
                s2 = s2 + (sx * sx) * even
                s3 = s3 + (sx * sx) * odd
            vy = jnp.full((row_count, cols), sy, f32)
            y2 = vy * vy
            a, b, cc, d, e, f, g, h = sums
            ys0 = vy * s0
            return (
                a + s0,
                b + s1,
                cc + ys0,
                d + s2,
                e + y2 * s0,
                f + vy * s1,
                g + s3 + y2 * s1,
                h + vy * s2 + y2 * ys0,
            )

        return lax.fori_loop(0, span, body, sums)

    def copy_out(c):
        return pltpu.make_async_copy(
            conv.at[pl.ds(c * span * VX, span * VX)],
            conv_out.at[pl.ds(c * span * VX, span * VX)],
            out_sem.at[c],
        )

    def reduce_copy(it, r):
        return pltpu.make_async_remote_copy(
            src_ref=part.at[it, r],
            dst_ref=gath.at[it, me],
            send_sem=rs_send.at[it, r],
            recv_sem=rs_recv.at[it, me],
            device_id={"vel": first_owner + r, "space": here},
            device_id_type=MESH,
        )

    def row_copy(it, p, other):
        low = mine < SWEEPS
        target = jnp.where(low, left, right)
        slot = jnp.where(low, mine + SWEEPS + row_count, mine - (row_count - SWEEPS))
        if not other:
            target, slot = here, mine + SWEEPS
        return pltpu.make_async_remote_copy(
            src_ref=row_send.at[it],
            dst_ref=rows.at[it, slot],
            send_sem=ag_send.at[it, other, p],
            recv_sem=ag_recv.at[it, slot],
            device_id={"vel": p, "space": target},
            device_id_type=MESH,
        )

    def reduce(it, sums):
        for k in range(8):
            part[it, :, k, :] = sums[k] * QUAD
        for r in range(row_count):

            @pl.when(me != first_owner + r)
            def _():
                reduce_copy(it, r).start()

        @pl.when(owner)
        def _():
            gath[it, me] = part[it, mine]

            def add(i, sums):
                @pl.when(i != me)
                def _():
                    pltpu.make_async_remote_copy(
                        src_ref=part.at[it, 0],
                        dst_ref=gath.at[it, i],
                        send_sem=rs_send.at[it, 0],
                        recv_sem=rs_recv.at[it, i],
                        device_id={"vel": i, "space": here},
                        device_id_type=MESH,
                    ).wait_recv()

                sz = speed_z(velocity_base(i, vel_count)[1])
                value = gath[it, i]
                v1 = sz * value
                v2 = sz * v1
                v3 = sz * v2
                return (sums[0] + value, sums[1] + v1, sums[2] + v2, sums[3] + v3)

            zero = jnp.zeros((8, cols), f32)
            total = lax.fori_loop(0, groups, add, (zero, zero, zero, zero))
            values = heat_row(*total)
            for k in range(8):
                row_send[it, pl.ds(k, 1), :] = values[k]
            rows[it, mine + SWEEPS] = row_send[it]

            def spread(p, carry):
                @pl.when(p != me)
                def _():
                    row_copy(it, p, 0).start()

                row_copy(it, p, 1).start()
                return carry

            lax.fori_loop(0, groups, spread, 0)

    def await_rows(it):
        for slot in range(row_count + 2 * SWEEPS):

            def wait():
                pltpu.make_async_remote_copy(
                    src_ref=row_send.at[it],
                    dst_ref=rows.at[it, slot],
                    send_sem=ag_send.at[it, 0, 0],
                    recv_sem=ag_recv.at[it, slot],
                    device_id={"vel": me, "space": right},
                    device_id_type=MESH,
                ).wait_recv()

            if SWEEPS <= slot < SWEEPS + row_count:
                pl.when(me != first_owner + slot - SWEEPS)(wait)
            else:
                wait()

    zero = jnp.zeros((row_count, cols), f32)
    for it in range(ITERS):
        if it == 0:
            for c in range(nch):
                for sign in range(2):
                    load_in(c, sign).wait()
                send_halo(it, c)
        else:
            await_rows(it - 1)
            diffuse_rows(rows.at[it - 1], tr, row_count)
            keep = macro_tables(tr, rate_ref, wall_ref, tab_x, tab_y, iy0, iz, iy_count)

            def load(iy, ix):
                return conv[iy * VX + ix]

            def store(iy, ix, value):
                sign, k = ix // HX, ix % HX
                pad[iy, sign, k, pl.ds(row_count * sign, row_count), :] = value

            for c in range(nch):
                collide(load, store, tab_x, tab_y, keep, c * span, span)
                send_halo(it, c)
        sums = (zero,) * 8
        for c in range(nch):
            take_halo(it, c)
            sums = transport(c, sums)
            if it == ITERS - 1:
                copy_out(c).start()
        reduce(it, sums)
    last = ITERS - 1
    await_rows(last)
    rows_copy = pltpu.make_async_copy(rows.at[last], rows_out, out_sem.at[nch])
    rows_copy.start()
    for it in range(ITERS):
        for c in range(nch):
            for sign in range(2):
                halo(it, c, sign).wait_send()
        for r in range(row_count):

            @pl.when(me != first_owner + r)
            def _():
                reduce_copy(it, r).wait_send()

        @pl.when(owner)
        def _():
            def drain(p, carry):
                @pl.when(p != me)
                def _():
                    row_copy(it, p, 0).wait_send()

                row_copy(it, p, 1).wait_send()
                return carry

            lax.fori_loop(0, groups, drain, 0)

    for c in range(nch):
        copy_out(c).wait()
    rows_copy.wait()


def final_kernel(
    conv_in, rows, rate_ref, wall_ref, out, fields, buf, tr, tab_x, tab_y, in_sem, out_sem
):
    vel_count, row_count, cols = conv_in.shape
    iy_count = vel_count // VX
    nch = chunks_of(iy_count)
    span = iy_count // nch
    iy0, iz = velocity_base(lax.axis_index("vel"), vel_count)

    def piece(c):
        return pl.ds(c * span * VX, span * VX)

    def load_in(c):
        return pltpu.make_async_copy(conv_in.at[piece(c)], buf.at[piece(c)], in_sem.at[c])

    def copy_out(c):
        return pltpu.make_async_copy(buf.at[piece(c)], out.at[piece(c)], out_sem.at[c])

    for c in range(nch):
        load_in(c).start()
    diffuse_rows(rows, tr, row_count)
    for k in range(5):
        fields[k] = tr[:, k, :]
    keep = macro_tables(tr, rate_ref, wall_ref, tab_x, tab_y, iy0, iz, iy_count)

    def load(iy, ix):
        return buf[iy * VX + ix]

    def store(iy, ix, value):
        buf[iy * VX + ix] = value

    for c in range(nch):
        load_in(c).wait()
        collide(load, store, tab_x, tab_y, keep, c * span, span)
        copy_out(c).start()
    for c in range(nch):
        copy_out(c).wait()


def per_device(groups, tiles, distribution, rate_class, boundary_obstacle_indicator):
    vel_count, row_count, cols = distribution.shape
    iy_count = vel_count // VX
    nch = chunks_of(iy_count)
    vmem = pl.BlockSpec(memory_space=pltpu.VMEM)
    anywhere = pl.BlockSpec(memory_space=pl.ANY)
    total = row_count + 2 * SWEEPS
    tile = (row_count, cols)
    dma = pltpu.SemaphoreType.DMA
    conv, rows = pl.pallas_call(
        functools.partial(advance_kernel, groups, tiles),
        out_shape=(
            jax.ShapeDtypeStruct(distribution.shape, f32),
            jax.ShapeDtypeStruct((total, 8, cols), f32),
        ),
        in_specs=[anywhere, vmem, vmem],
        out_specs=(anywhere, anywhere),
        scratch_shapes=[
            pltpu.VMEM((iy_count, 2, HX, 2 * row_count, cols), f32),
            pltpu.VMEM((vel_count,) + tile, f32),
            pltpu.VMEM((ITERS, 2, iy_count, HX, cols), f32),
            pltpu.VMEM((ITERS, 2, iy_count, HX, cols), f32),
            pltpu.VMEM((ITERS, row_count, 8, cols), f32),
            pltpu.VMEM((ITERS, groups, 8, cols), f32),
            pltpu.VMEM((ITERS, 8, cols), f32),
            pltpu.VMEM((ITERS, total, 8, cols), f32),
            pltpu.VMEM((row_count, 8, cols), f32),
            pltpu.VMEM((3, VX) + tile, f32),
            pltpu.VMEM((3, iy_count) + tile, f32),
            dma((nch, 2)),
            dma((nch + 1,)),
            dma((ITERS, 2, nch)),
            dma((ITERS, 2, nch)),
            dma((ITERS, row_count)),
            dma((ITERS, groups)),
            dma((ITERS, 2, groups)),
            dma((ITERS, total)),
        ],
        compiler_params=pltpu.CompilerParams(collective_id=0, has_side_effects=True),
    )(
        distribution.reshape(iy_count, 2, HX, row_count, cols),
        rate_class,
        boundary_obstacle_indicator,
    )
    field, fields = pl.pallas_call(
        final_kernel,
        out_shape=(
            jax.ShapeDtypeStruct(distribution.shape, f32),
            jax.ShapeDtypeStruct((5,) + tile, f32),
        ),
        in_specs=[anywhere, vmem, vmem, vmem],
        out_specs=(anywhere, vmem),
        scratch_shapes=[
            pltpu.VMEM((vel_count,) + tile, f32),
            pltpu.VMEM((row_count, 8, cols), f32),
            pltpu.VMEM((3, VX) + tile, f32),
            pltpu.VMEM((3, iy_count) + tile, f32),
            dma((nch,)),
            dma((nch,)),
        ],
    )(conv, rows, rate_class, boundary_obstacle_indicator)
    return field, fields


def solution(mesh):
    placed = (P("vel", "space", None), P("space", None), P("space", None))
    return jax.shard_map(
        functools.partial(per_device, mesh.shape["vel"], mesh.shape["space"]),
        mesh=mesh,
        in_specs=placed,
        out_specs=(P("vel", "space", None), P(None, "space", None)),
        check_vma=False,
    )
```

```python
import functools

import jax
import jax.numpy as jnp
from jax import lax
from jax.experimental import pallas as pl
from jax.experimental.pallas import tpu as pltpu
from jax.sharding import PartitionSpec as P

VX = 32
VY = 32
VZ = 16
HX = VX // 2
ITERS = 2
SWEEPS = 4
EDGE = 5.0
STEP = 0.1
PRANDTL = 2.0 / 3.0
SHEAR = 0.81
DIFFUSIVITY = 1.0
QUAD = (
    (2.0 * EDGE / VX) * (2.0 * EDGE / VY) * (2.0 * EDGE / VZ) / (2.0 * 3.141592653589793) ** 1.5
)
MESH = pl.DeviceIdType.MESH
f32 = jnp.float32


def speed_x(ix):
    return -EDGE + (ix + 0.5) * (2.0 * EDGE / VX)


def speed_y(iy):
    return -EDGE + (iy.astype(f32) + 0.5) * (2.0 * EDGE / VY)


def speed_z(iz):
    return -EDGE + (iz.astype(f32) + 0.5) * (2.0 * EDGE / VZ)


def velocity_base(vel_index, vel_count):
    first = vel_index * vel_count
    return lax.rem(lax.div(first, VX), VY), lax.div(first, VX * VY)


def diffuse_rows(rows_ref, tr_ref, row_count):
    total = row_count + 2 * SWEEPS
    src = [rows_ref[i] for i in range(total)]
    cols = src[0].shape[1]
    state = list(src)
    for sweep in range(SWEEPS):
        new = list(state)
        for i in range(sweep + 1, total - sweep - 1):
            beside = (
                state[i - 1]
                + state[i + 1]
                + pltpu.roll(state[i], 1, 1)
                + pltpu.roll(state[i], cols - 1, 1)
            )
            new[i] = (src[i] + DIFFUSIVITY * beside) * (1.0 / (1.0 + 4.0 * DIFFUSIVITY))
        state = new
    sub = lax.broadcasted_iota(jnp.int32, src[0].shape, 0)
    for r in range(row_count):
        tr_ref[r] = jnp.where(sub < 5, state[SWEEPS + r], src[SWEEPS + r])


def macro_tables(tr_ref, rate_ref, wall_ref, tab_x, tab_y, iy0, iz, iy_count):
    q = [tr_ref[:, k, :] for k in range(8)]
    density = q[0]
    inv_density = 1.0 / density
    ux, uy, uz = q[1] * inv_density, q[2] * inv_density, q[3] * inv_density
    temperature = (2.0 * q[4] * inv_density - (ux * ux + uy * uy + uz * uz)) / 3.0
    frequency = 0.5 * jnp.exp2(rate_ref[...].astype(f32))
    power = jnp.exp((1.0 - SHEAR) * jnp.log(temperature))
    rate = 1.0 - jnp.exp(-STEP * frequency * density * power)
    wall = wall_ref[...] > 0
    inv_t = 1.0 / temperature
    root = lax.rsqrt(temperature)
    prefactor = density * (root * root * root)
    coef = (1.0 - PRANDTL) / (5.0 * density * temperature * temperature)
    hx, hy, hz = coef * q[5], coef * q[6], coef * q[7]
    zero = jnp.zeros_like(density)
    sz = jnp.full(density.shape, speed_z(iz), f32)
    cz = sz - uz
    z2 = cz * cz * inv_t
    scale_z = rate * prefactor * jnp.exp(-0.5 * z2)
    wall_z = density * jnp.exp(-0.5 * sz * sz)
    qz = hz * cz

    def table_x(ix, carry):
        sx = jnp.full(density.shape, speed_x(ix.astype(f32)), f32)
        cx = sx - ux
        x2 = cx * cx * inv_t
        tab_x[0, ix] = jnp.exp(-0.5 * jnp.where(wall, sx * sx, x2))
        tab_x[1, ix] = jnp.where(wall, zero, hx * cx)
        tab_x[2, ix] = jnp.where(wall, zero, x2)
        return carry

    lax.fori_loop(0, VX, table_x, 0, unroll=4)

    def table_y(iy, carry):
        sy = jnp.full(density.shape, speed_y(iy0 + iy), f32)
        cy = sy - uy
        y2 = cy * cy * inv_t
        tab_y[0, iy] = jnp.where(wall, wall_z, scale_z) * jnp.exp(
            -0.5 * jnp.where(wall, sy * sy, y2)
        )
        tab_y[1, iy] = jnp.where(wall, zero, hy * cy + qz)
        tab_y[2, iy] = jnp.where(wall, zero, y2 + z2 - 5.0)
        return carry

    lax.fori_loop(0, iy_count, table_y, 0, unroll=min(4, iy_count))
    return jnp.where(wall, zero, 1.0 - rate)


def collide(load, store, tab_x, tab_y, keep, start, count):
    block = 4 if count % 4 == 0 else 2 if count % 2 == 0 else 1

    def body(step, carry):
        base = start + step * block
        g = [tab_y[0, base + b] for b in range(block)]
        h = [tab_y[1, base + b] for b in range(block)]
        r = [tab_y[2, base + b] for b in range(block)]
        for ix in range(VX):
            ex, ax, bx = tab_x[0, ix], tab_x[1, ix], tab_x[2, ix]
            for b in range(block):
                old = load(base + b, ix)
                shape = (ax + h[b]) * (bx + r[b]) + 1.0
                store(base + b, ix, keep * old + (ex * g[b]) * shape)
        return carry

    lax.fori_loop(0, count // block, body, 0)


def chunks_of(iy_count):
    return 4 if iy_count % 4 == 0 else 1


def heat_row(total, z1, z2, z3):
    def at(array, k):
        return array[k : k + 1, :]

    m0, m1, m2, m3 = at(total, 0), at(total, 1), at(total, 2), at(z1, 0)
    m5, m6, m7 = at(total, 3), at(total, 4), at(total, 5)
    m4 = m5 + m6 + at(z2, 0)
    m8, m9 = at(z1, 1), at(z1, 2)
    m10 = at(total, 6) + at(z2, 1)
    m11 = at(total, 7) + at(z2, 2)
    m12 = at(z1, 3) + at(z1, 4) + at(z3, 0)
    inv = 1.0 / m0
    ux, uy, uz = m1 * inv, m2 * inv, m3 * inv
    pzz = at(z2, 0)
    extra = 2.0 * m0 * (ux * ux + uy * uy + uz * uz) - m4
    heat_x = 0.5 * (m10 - 2.0 * (ux * m5 + uy * m7 + uz * m8) + extra * ux)
    heat_y = 0.5 * (m11 - 2.0 * (ux * m7 + uy * m6 + uz * m9) + extra * uy)
    heat_z = 0.5 * (m12 - 2.0 * (ux * m8 + uy * m9 + uz * pzz) + extra * uz)
    return [m0, m1, m2, m3, 0.5 * m4, heat_x, heat_y, heat_z]


def advance_kernel(
    groups,
    tiles,
    dist,
    rate_ref,
    wall_ref,
    conv_out,
    rows_out,
    pad,
    conv,
    hal_send,
    hal_recv,
    part,
    gath,
    row_send,
    rows,
    tr,
    tab_x,
    tab_y,
    in_sem,
    out_sem,
    hs_sem,
    hr_sem,
    rs_send,
    rs_recv,
    ag_send,
    ag_recv,
):
    iy_count, _, _, row_count, cols = dist.shape
    vel_count = iy_count * VX
    nch = chunks_of(iy_count)
    span = iy_count // nch
    me = lax.axis_index("vel")
    here = lax.axis_index("space")
    right = lax.rem(here + 1, tiles)
    left = lax.rem(here + tiles - 1, tiles)
    iy0, iz = velocity_base(me, vel_count)
    first_owner = groups // 2 - row_count // 2
    mine = me - first_owner
    owner = jnp.logical_and(mine >= 0, mine < row_count)

    def load_in(c, sign):
        lo = row_count * sign
        return pltpu.make_async_copy(
            dist.at[pl.ds(c * span, span), sign],
            pad.at[pl.ds(c * span, span), sign, :, pl.ds(lo, row_count), :],
            in_sem.at[c, sign],
        )

    for c in range(nch):
        for sign in range(2):
            load_in(c, sign).start()

    barrier = pltpu.get_barrier_semaphore()

    def greet(p, carry):
        @pl.when(p != me)
        def _():
            pl.semaphore_signal(
                barrier, inc=1, device_id={"vel": p, "space": here}, device_id_type=MESH
            )

        for other in (left, right):
            pl.semaphore_signal(
                barrier, inc=1, device_id={"vel": p, "space": other}, device_id_type=MESH
            )
        return carry

    lax.fori_loop(0, groups, greet, 0)
    flat_pad = pad.reshape(vel_count * 2 * row_count, cols)
    flat_conv = conv.reshape(vel_count * row_count, cols)

    def pad_rows(iy, sign, k, row):
        start = ((iy * 2 + sign) * HX + k) * 2 * row_count + row
        return pl.ds(start, 8, stride=2 * row_count)

    def clear(iy, carry):
        for sign in range(2):
            for k in range(0, HX, 8):
                row = row_count - 1 if sign else row_count
                flat_pad[pad_rows(iy, sign, k, row), :] = jnp.zeros((8, cols), f32)
        return carry

    lax.fori_loop(0, iy_count, clear, 0)

    def halo(it, c, sign):
        return pltpu.make_async_remote_copy(
            src_ref=hal_send.at[it, sign, pl.ds(c * span, span)],
            dst_ref=hal_recv.at[it, sign, pl.ds(c * span, span)],
            send_sem=hs_sem.at[it, sign, c],
            recv_sem=hr_sem.at[it, sign, c],
            device_id={"vel": me, "space": right if sign else left},
            device_id_type=MESH,
        )

    def pack_halo(it, c):
        def pack(j, carry):
            iy = c * span + j
            for sign in range(2):
                row = 2 * row_count - 1 if sign else 0
                for k in range(0, HX, 8):
                    hal_send[it, sign, iy, pl.ds(k, 8), :] = flat_pad[
                        pad_rows(iy, sign, k, row), :
                    ]
            return carry

        lax.fori_loop(0, span, pack, 0)

    def send_halo(it, c):
        for sign in range(2):
            halo(it, c, sign).start()

    sub = lax.broadcasted_iota(jnp.int32, (8, cols), 0)
    groups_x = [(sign, k) for sign in range(2) for k in range(0, HX, 8)]
    group_sx = [speed_x((sub + (sign * HX + k)).astype(f32)) for sign, k in groups_x]

    def fix_halo(it, c, carry):
        for sign in range(2):
            halo(it, c, sign).wait_recv()

        def body(j, carry):
            iy = c * span + j
            sy = jnp.full((8, cols), speed_y(iy0 + iy), f32)
            out = []
            for n, (sign, k) in enumerate(groups_x):
                row = 0 if sign else row_count - 1
                extra = STEP * jnp.abs(group_sx[n]) * hal_recv[it, sign, iy, pl.ds(k, 8), :]
                where = pl.ds((iy * VX + sign * HX + k) * row_count + row, 8, stride=row_count)
                flat_conv[where, :] = flat_conv[where, :] + extra
                e1 = sy * extra
                e2 = sy * e1
                u = carry[n]
                out.append((u[0] + extra, u[1] + e1, u[2] + e2, u[3] + sy * e2))
            return tuple(out)

        return lax.fori_loop(0, span, body, carry)

    def add_fix(sums, carry):
        rows_of = lax.broadcasted_iota(jnp.int32, (row_count, cols), 0)
        for sign in range(2):
            parts = [[] for _ in range(8)]
            for n, (group_sign, _) in enumerate(groups_x):
                if group_sign != sign:
                    continue
                x, (u0, u1, u2, u3) = group_sx[n], carry[n]
                x0 = x * u0
                xx0 = x * x0
                values = (u0, x0, u1, xx0, u2, x * u1, x * (xx0 + u2), x * (x * u1) + u3)
                for k in range(8):
                    parts[k].append(values[k])
            target = 0 if sign else row_count - 1
            sums = tuple(
                old + jnp.where(rows_of == target, jnp.sum(sum(p), axis=0, keepdims=True), 0.0)
                for old, p in zip(sums, parts)
            )
        return sums

    def transport(c, sums):
        def body(j, sums):
            iy = c * span + j
            iyg = iy0 + iy
            sy = speed_y(iyg)
            cy = jnp.full((row_count, cols), STEP * jnp.abs(sy), f32)
            shift = jnp.where(iyg < VY // 2, cols - 1, 1).astype(jnp.int32)

            def moved(ix):
                sign, k = ix // HX, ix % HX
                lo = row_count * sign
                cur = pad[iy, sign, k, pl.ds(lo, row_count), :]
                near = pad[iy, sign, k, pl.ds(lo - 1 if sign else lo + 1, row_count), :]
                along = pltpu.roll(cur, shift, 1)
                cx = STEP * abs(speed_x(ix))
                new = cur + cx * (near - cur) + cy * (along - cur)
                conv[iy * VX + ix] = new
                return new

            s0 = s1 = s2 = s3 = jnp.zeros((row_count, cols), f32)
            for k in range(HX):
                low, high = moved(k), moved(VX - 1 - k)
                sx = speed_x(VX - 1 - k)
                even, odd = high + low, sx * (high - low)
                s0 = s0 + even
                s1 = s1 + odd
                s2 = s2 + (sx * sx) * even
                s3 = s3 + (sx * sx) * odd
            vy = jnp.full((row_count, cols), sy, f32)
            y2 = vy * vy
            a, b, cc, d, e, f, g, h = sums
            ys0 = vy * s0
            return (
                a + s0,
                b + s1,
                cc + ys0,
                d + s2,
                e + y2 * s0,
                f + vy * s1,
                g + s3 + y2 * s1,
                h + vy * s2 + y2 * ys0,
            )

        return lax.fori_loop(0, span, body, sums)

    def copy_out(c):
        return pltpu.make_async_copy(
            conv.at[pl.ds(c * span * VX, span * VX)],
            conv_out.at[pl.ds(c * span * VX, span * VX)],
            out_sem.at[c],
        )

    def reduce_copy(it, r):
        return pltpu.make_async_remote_copy(
            src_ref=part.at[it, r],
            dst_ref=gath.at[it, me],
            send_sem=rs_send.at[it, r],
            recv_sem=rs_recv.at[it, me],
            device_id={"vel": first_owner + r, "space": here},
            device_id_type=MESH,
        )

    def row_copy(it, p, other):
        low = mine < SWEEPS
        target = jnp.where(low, left, right)
        slot = jnp.where(low, mine + SWEEPS + row_count, mine - (row_count - SWEEPS))
        if not other:
            target, slot = here, mine + SWEEPS
        return pltpu.make_async_remote_copy(
            src_ref=row_send.at[it],
            dst_ref=rows.at[it, slot],
            send_sem=ag_send.at[it, other, p],
            recv_sem=ag_recv.at[it, slot],
            device_id={"vel": p, "space": target},
            device_id_type=MESH,
        )

    def reduce(it, sums):
        for k in range(8):
            part[it, :, k, :] = sums[k] * QUAD
        for r in range(row_count):

            @pl.when(me != first_owner + r)
            def _():
                reduce_copy(it, r).start()

        @pl.when(owner)
        def _():
            gath[it, me] = part[it, mine]

            def add(i, sums):
                @pl.when(i != me)
                def _():
                    pltpu.make_async_remote_copy(
                        src_ref=part.at[it, 0],
                        dst_ref=gath.at[it, i],
                        send_sem=rs_send.at[it, 0],
                        recv_sem=rs_recv.at[it, i],
                        device_id={"vel": i, "space": here},
                        device_id_type=MESH,
                    ).wait_recv()

                sz = speed_z(velocity_base(i, vel_count)[1])
                value = gath[it, i]
                v1 = sz * value
                v2 = sz * v1
                v3 = sz * v2
                return (sums[0] + value, sums[1] + v1, sums[2] + v2, sums[3] + v3)

            zero = jnp.zeros((8, cols), f32)
            total = lax.fori_loop(0, groups, add, (zero, zero, zero, zero))
            values = heat_row(*total)
            for k in range(8):
                row_send[it, pl.ds(k, 1), :] = values[k]
            rows[it, mine + SWEEPS] = row_send[it]

            def spread(p, carry):
                @pl.when(p != me)
                def _():
                    row_copy(it, p, 0).start()

                row_copy(it, p, 1).start()
                return carry

            lax.fori_loop(0, groups, spread, 0)

    def await_rows(it):
        for slot in range(row_count + 2 * SWEEPS):

            def wait():
                pltpu.make_async_remote_copy(
                    src_ref=row_send.at[it],
                    dst_ref=rows.at[it, slot],
                    send_sem=ag_send.at[it, 0, 0],
                    recv_sem=ag_recv.at[it, slot],
                    device_id={"vel": me, "space": right},
                    device_id_type=MESH,
                ).wait_recv()

            if SWEEPS <= slot < SWEEPS + row_count:
                pl.when(me != first_owner + slot - SWEEPS)(wait)
            else:
                wait()

    zero = jnp.zeros((row_count, cols), f32)
    zero8 = jnp.zeros((8, cols), f32)
    ready = nch // 2
    for it in range(ITERS):
        sums = (zero,) * 8
        if it == 0:
            for c in range(nch):
                if c <= ready:
                    arrived = range(c, nch) if c == ready else (c,)
                    for d in arrived:
                        for sign in range(2):
                            load_in(d, sign).wait()
                        pack_halo(it, d)
                if c == ready:
                    pl.semaphore_wait(barrier, 3 * groups - 1)
                    for d in range(nch):
                        send_halo(it, d)
                sums = transport(c, sums)
        else:
            await_rows(it - 1)
            diffuse_rows(rows.at[it - 1], tr, row_count)
            keep = macro_tables(tr, rate_ref, wall_ref, tab_x, tab_y, iy0, iz, iy_count)

            def load(iy, ix):
                return conv[iy * VX + ix]

            def store(iy, ix, value):
                sign, k = ix // HX, ix % HX
                pad[iy, sign, k, pl.ds(row_count * sign, row_count), :] = value

            for c in range(nch):
                collide(load, store, tab_x, tab_y, keep, c * span, span)
                pack_halo(it, c)
                send_halo(it, c)
                sums = transport(c, sums)
        added = ((zero8,) * 4,) * len(groups_x)
        for c in range(nch):
            added = fix_halo(it, c, added)
            if it == ITERS - 1:
                copy_out(c).start()
        reduce(it, add_fix(sums, added))
    last = ITERS - 1
    await_rows(last)
    rows_copy = pltpu.make_async_copy(rows.at[last], rows_out, out_sem.at[nch])
    rows_copy.start()
    for it in range(ITERS):
        for c in range(nch):
            for sign in range(2):
                halo(it, c, sign).wait_send()
        for r in range(row_count):

            @pl.when(me != first_owner + r)
            def _():
                reduce_copy(it, r).wait_send()

        @pl.when(owner)
        def _():
            def drain(p, carry):
                @pl.when(p != me)
                def _():
                    row_copy(it, p, 0).wait_send()

                row_copy(it, p, 1).wait_send()
                return carry

            lax.fori_loop(0, groups, drain, 0)

    for c in range(nch):
        copy_out(c).wait()
    rows_copy.wait()


def final_kernel(
    conv_in, rows, rate_ref, wall_ref, out, fields, buf, tr, tab_x, tab_y, in_sem, out_sem
):
    vel_count, row_count, cols = conv_in.shape
    iy_count = vel_count // VX
    nch = chunks_of(iy_count)
    span = iy_count // nch
    iy0, iz = velocity_base(lax.axis_index("vel"), vel_count)

    def piece(c):
        return pl.ds(c * span * VX, span * VX)

    def load_in(c):
        return pltpu.make_async_copy(conv_in.at[piece(c)], buf.at[piece(c)], in_sem.at[c])

    def copy_out(c):
        return pltpu.make_async_copy(buf.at[piece(c)], out.at[piece(c)], out_sem.at[c])

    for c in range(nch):
        load_in(c).start()
    diffuse_rows(rows, tr, row_count)
    for k in range(5):
        fields[k] = tr[:, k, :]
    keep = macro_tables(tr, rate_ref, wall_ref, tab_x, tab_y, iy0, iz, iy_count)

    def load(iy, ix):
        return buf[iy * VX + ix]

    def store(iy, ix, value):
        buf[iy * VX + ix] = value

    for c in range(nch):
        load_in(c).wait()
        collide(load, store, tab_x, tab_y, keep, c * span, span)
        copy_out(c).start()
    for c in range(nch):
        copy_out(c).wait()


def per_device(groups, tiles, distribution, rate_class, boundary_obstacle_indicator):
    vel_count, row_count, cols = distribution.shape
    iy_count = vel_count // VX
    nch = chunks_of(iy_count)
    vmem = pl.BlockSpec(memory_space=pltpu.VMEM)
    anywhere = pl.BlockSpec(memory_space=pl.ANY)
    total = row_count + 2 * SWEEPS
    tile = (row_count, cols)
    dma = pltpu.SemaphoreType.DMA
    conv, rows = pl.pallas_call(
        functools.partial(advance_kernel, groups, tiles),
        out_shape=(
            jax.ShapeDtypeStruct(distribution.shape, f32),
            jax.ShapeDtypeStruct((total, 8, cols), f32),
        ),
        in_specs=[anywhere, vmem, vmem],
        out_specs=(anywhere, anywhere),
        scratch_shapes=[
            pltpu.VMEM((iy_count, 2, HX, 2 * row_count, cols), f32),
            pltpu.VMEM((vel_count,) + tile, f32),
            pltpu.VMEM((ITERS, 2, iy_count, HX, cols), f32),
            pltpu.VMEM((ITERS, 2, iy_count, HX, cols), f32),
            pltpu.VMEM((ITERS, row_count, 8, cols), f32),
            pltpu.VMEM((ITERS, groups, 8, cols), f32),
            pltpu.VMEM((ITERS, 8, cols), f32),
            pltpu.VMEM((ITERS, total, 8, cols), f32),
            pltpu.VMEM((row_count, 8, cols), f32),
            pltpu.VMEM((3, VX) + tile, f32),
            pltpu.VMEM((3, iy_count) + tile, f32),
            dma((nch, 2)),
            dma((nch + 1,)),
            dma((ITERS, 2, nch)),
            dma((ITERS, 2, nch)),
            dma((ITERS, row_count)),
            dma((ITERS, groups)),
            dma((ITERS, 2, groups)),
            dma((ITERS, total)),
        ],
        compiler_params=pltpu.CompilerParams(collective_id=0, has_side_effects=True),
    )(
        distribution.reshape(iy_count, 2, HX, row_count, cols),
        rate_class,
        boundary_obstacle_indicator,
    )
    field, fields = pl.pallas_call(
        final_kernel,
        out_shape=(
            jax.ShapeDtypeStruct(distribution.shape, f32),
            jax.ShapeDtypeStruct((5,) + tile, f32),
        ),
        in_specs=[anywhere, vmem, vmem, vmem],
        out_specs=(anywhere, vmem),
        scratch_shapes=[
            pltpu.VMEM((vel_count,) + tile, f32),
            pltpu.VMEM((row_count, 8, cols), f32),
            pltpu.VMEM((3, VX) + tile, f32),
            pltpu.VMEM((3, iy_count) + tile, f32),
            dma((nch,)),
            dma((nch,)),
        ],
    )(conv, rows, rate_class, boundary_obstacle_indicator)
    return field, fields


def solution(mesh):
    placed = (P("vel", "space", None), P("space", None), P("space", None))
    return jax.shard_map(
        functools.partial(per_device, mesh.shape["vel"], mesh.shape["space"]),
        mesh=mesh,
        in_specs=placed,
        out_specs=(P("vel", "space", None), P(None, "space", None)),
        check_vma=False,
    )
```

```python
import functools

import jax
import jax.numpy as jnp
from jax import lax
from jax.experimental import pallas as pl
from jax.experimental.pallas import tpu as pltpu
from jax.sharding import PartitionSpec as P

VX = 32
VY = 32
VZ = 16
HX = VX // 2
ITERS = 2
SWEEPS = 4
EDGE = 5.0
STEP = 0.1
PRANDTL = 2.0 / 3.0
SHEAR = 0.81
DIFFUSIVITY = 1.0
QUAD = (
    (2.0 * EDGE / VX) * (2.0 * EDGE / VY) * (2.0 * EDGE / VZ) / (2.0 * 3.141592653589793) ** 1.5
)
MESH = pl.DeviceIdType.MESH
f32 = jnp.float32


def speed_x(ix):
    return -EDGE + (ix + 0.5) * (2.0 * EDGE / VX)


def speed_y(iy):
    return -EDGE + (iy.astype(f32) + 0.5) * (2.0 * EDGE / VY)


def speed_z(iz):
    return -EDGE + (iz.astype(f32) + 0.5) * (2.0 * EDGE / VZ)


def velocity_base(vel_index, vel_count):
    first = vel_index * vel_count
    return lax.rem(lax.div(first, VX), VY), lax.div(first, VX * VY)


def diffuse_rows(rows_ref, tr_ref, row_count):
    total = row_count + 2 * SWEEPS
    src = [rows_ref[i] for i in range(total)]
    cols = src[0].shape[1]
    state = list(src)
    for sweep in range(SWEEPS):
        new = list(state)
        for i in range(sweep + 1, total - sweep - 1):
            beside = (
                state[i - 1]
                + state[i + 1]
                + pltpu.roll(state[i], 1, 1)
                + pltpu.roll(state[i], cols - 1, 1)
            )
            new[i] = (src[i] + DIFFUSIVITY * beside) * (1.0 / (1.0 + 4.0 * DIFFUSIVITY))
        state = new
    sub = lax.broadcasted_iota(jnp.int32, src[0].shape, 0)
    for r in range(row_count):
        tr_ref[r] = jnp.where(sub < 5, state[SWEEPS + r], src[SWEEPS + r])


def macro_tables(tr_ref, rate_ref, wall_ref, tab_x, tab_y, iy0, iz, iy_count):
    q = [tr_ref[:, k, :] for k in range(8)]
    density = q[0]
    inv_density = 1.0 / density
    ux, uy, uz = q[1] * inv_density, q[2] * inv_density, q[3] * inv_density
    temperature = (2.0 * q[4] * inv_density - (ux * ux + uy * uy + uz * uz)) / 3.0
    frequency = 0.5 * jnp.exp2(rate_ref[...].astype(f32))
    power = jnp.exp((1.0 - SHEAR) * jnp.log(temperature))
    rate = 1.0 - jnp.exp(-STEP * frequency * density * power)
    wall = wall_ref[...] > 0
    inv_t = 1.0 / temperature
    root = lax.rsqrt(temperature)
    prefactor = density * (root * root * root)
    coef = (1.0 - PRANDTL) / (5.0 * density * temperature * temperature)
    hx, hy, hz = coef * q[5], coef * q[6], coef * q[7]
    zero = jnp.zeros_like(density)
    sz = jnp.full(density.shape, speed_z(iz), f32)
    cz = sz - uz
    z2 = cz * cz * inv_t
    scale_z = rate * prefactor * jnp.exp(-0.5 * z2)
    wall_z = density * jnp.exp(-0.5 * sz * sz)
    qz = hz * cz

    def table_x(ix, carry):
        sx = jnp.full(density.shape, speed_x(ix.astype(f32)), f32)
        cx = sx - ux
        x2 = cx * cx * inv_t
        tab_x[0, ix] = jnp.exp(-0.5 * jnp.where(wall, sx * sx, x2))
        tab_x[1, ix] = jnp.where(wall, zero, hx * cx)
        tab_x[2, ix] = jnp.where(wall, zero, x2)
        return carry

    lax.fori_loop(0, VX, table_x, 0, unroll=16)

    def table_y(iy, carry):
        sy = jnp.full(density.shape, speed_y(iy0 + iy), f32)
        cy = sy - uy
        y2 = cy * cy * inv_t
        tab_y[0, iy] = jnp.where(wall, wall_z, scale_z) * jnp.exp(
            -0.5 * jnp.where(wall, sy * sy, y2)
        )
        tab_y[1, iy] = jnp.where(wall, zero, hy * cy + qz)
        tab_y[2, iy] = jnp.where(wall, zero, y2 + z2 - 5.0)
        return carry

    lax.fori_loop(0, iy_count, table_y, 0, unroll=min(16, iy_count))
    return jnp.where(wall, zero, 1.0 - rate)


def collide(load, store, tab_x, tab_y, keep, start, count):
    block = 4 if count % 4 == 0 else 2 if count % 2 == 0 else 1

    def body(step, carry):
        base = start + step * block
        g = [tab_y[0, base + b] for b in range(block)]
        h = [tab_y[1, base + b] for b in range(block)]
        r = [tab_y[2, base + b] for b in range(block)]
        for ix in range(VX):
            ex, ax, bx = tab_x[0, ix], tab_x[1, ix], tab_x[2, ix]
            for b in range(block):
                old = load(base + b, ix)
                shape = (ax + h[b]) * (bx + r[b]) + 1.0
                store(base + b, ix, keep * old + (ex * g[b]) * shape)
        return carry

    lax.fori_loop(0, count // block, body, 0)


def chunks_of(iy_count):
    return 4 if iy_count % 4 == 0 else 1


def heat_row(total, z1, z2, z3):
    def at(array, k):
        return array[k : k + 1, :]

    m0, m1, m2, m3 = at(total, 0), at(total, 1), at(total, 2), at(z1, 0)
    m5, m6, m7 = at(total, 3), at(total, 4), at(total, 5)
    m4 = m5 + m6 + at(z2, 0)
    m8, m9 = at(z1, 1), at(z1, 2)
    m10 = at(total, 6) + at(z2, 1)
    m11 = at(total, 7) + at(z2, 2)
    m12 = at(z1, 3) + at(z1, 4) + at(z3, 0)
    inv = 1.0 / m0
    ux, uy, uz = m1 * inv, m2 * inv, m3 * inv
    pzz = at(z2, 0)
    extra = 2.0 * m0 * (ux * ux + uy * uy + uz * uz) - m4
    heat_x = 0.5 * (m10 - 2.0 * (ux * m5 + uy * m7 + uz * m8) + extra * ux)
    heat_y = 0.5 * (m11 - 2.0 * (ux * m7 + uy * m6 + uz * m9) + extra * uy)
    heat_z = 0.5 * (m12 - 2.0 * (ux * m8 + uy * m9 + uz * pzz) + extra * uz)
    return [m0, m1, m2, m3, 0.5 * m4, heat_x, heat_y, heat_z]


def advance_kernel(
    groups,
    tiles,
    dist,
    rate_ref,
    wall_ref,
    conv_out,
    rows_out,
    pad,
    conv,
    hal_send,
    hal_recv,
    part,
    gath,
    row_send,
    rows,
    tr,
    tab_x,
    tab_y,
    in_sem,
    out_sem,
    hs_sem,
    hr_sem,
    rs_send,
    rs_recv,
    ag_send,
    ag_recv,
):
    iy_count, _, _, row_count, cols = dist.shape
    vel_count = iy_count * VX
    nch = chunks_of(iy_count)
    span = iy_count // nch
    me = lax.axis_index("vel")
    here = lax.axis_index("space")
    right = lax.rem(here + 1, tiles)
    left = lax.rem(here + tiles - 1, tiles)
    iy0, iz = velocity_base(me, vel_count)
    first_owner = groups // 2 - row_count // 2
    mine = me - first_owner
    owner = jnp.logical_and(mine >= 0, mine < row_count)

    def load_in(c, sign):
        lo = row_count * sign
        return pltpu.make_async_copy(
            dist.at[pl.ds(c * span, span), sign],
            pad.at[pl.ds(c * span, span), sign, :, pl.ds(lo, row_count), :],
            in_sem.at[c, sign],
        )

    for c in range(nch):
        for sign in range(2):
            load_in(c, sign).start()

    barrier = pltpu.get_barrier_semaphore()

    def greet(p, carry):
        @pl.when(p != me)
        def _():
            pl.semaphore_signal(
                barrier, inc=1, device_id={"vel": p, "space": here}, device_id_type=MESH
            )

        for other in (left, right):
            pl.semaphore_signal(
                barrier, inc=1, device_id={"vel": p, "space": other}, device_id_type=MESH
            )
        return carry

    lax.fori_loop(0, groups, greet, 0)
    flat_pad = pad.reshape(vel_count * 2 * row_count, cols)
    flat_conv = conv.reshape(vel_count * row_count, cols)

    def pad_rows(iy, sign, k, row):
        start = ((iy * 2 + sign) * HX + k) * 2 * row_count + row
        return pl.ds(start, 8, stride=2 * row_count)

    def clear(iy, carry):
        for sign in range(2):
            for k in range(0, HX, 8):
                row = row_count - 1 if sign else row_count
                flat_pad[pad_rows(iy, sign, k, row), :] = jnp.zeros((8, cols), f32)
        return carry

    lax.fori_loop(0, iy_count, clear, 0)

    def halo(it, c, sign):
        return pltpu.make_async_remote_copy(
            src_ref=hal_send.at[it, sign, pl.ds(c * span, span)],
            dst_ref=hal_recv.at[it, sign, pl.ds(c * span, span)],
            send_sem=hs_sem.at[it, sign, c],
            recv_sem=hr_sem.at[it, sign, c],
            device_id={"vel": me, "space": right if sign else left},
            device_id_type=MESH,
        )

    def pack_halo(it, c):
        def pack(j, carry):
            iy = c * span + j
            for sign in range(2):
                row = 2 * row_count - 1 if sign else 0
                for k in range(0, HX, 8):
                    hal_send[it, sign, iy, pl.ds(k, 8), :] = flat_pad[
                        pad_rows(iy, sign, k, row), :
                    ]
            return carry

        lax.fori_loop(0, span, pack, 0, unroll=min(4, span))

    def send_halo(it, c):
        for sign in range(2):
            halo(it, c, sign).start()

    sub = lax.broadcasted_iota(jnp.int32, (8, cols), 0)
    groups_x = [(sign, k) for sign in range(2) for k in range(0, HX, 8)]
    group_sx = [speed_x((sub + (sign * HX + k)).astype(f32)) for sign, k in groups_x]

    def fix_halo(it, c, carry):
        for sign in range(2):
            halo(it, c, sign).wait_recv()

        def body(j, carry):
            iy = c * span + j
            sy = jnp.full((8, cols), speed_y(iy0 + iy), f32)
            out = []
            for n, (sign, k) in enumerate(groups_x):
                row = 0 if sign else row_count - 1
                extra = STEP * jnp.abs(group_sx[n]) * hal_recv[it, sign, iy, pl.ds(k, 8), :]
                where = pl.ds((iy * VX + sign * HX + k) * row_count + row, 8, stride=row_count)
                flat_conv[where, :] = flat_conv[where, :] + extra
                e1 = sy * extra
                e2 = sy * e1
                u = carry[n]
                out.append((u[0] + extra, u[1] + e1, u[2] + e2, u[3] + sy * e2))
            return tuple(out)

        return lax.fori_loop(0, span, body, carry, unroll=2)

    def add_fix(sums, carry):
        rows_of = lax.broadcasted_iota(jnp.int32, (row_count, cols), 0)
        for sign in range(2):
            parts = [[] for _ in range(8)]
            for n, (group_sign, _) in enumerate(groups_x):
                if group_sign != sign:
                    continue
                x, (u0, u1, u2, u3) = group_sx[n], carry[n]
                x0 = x * u0
                xx0 = x * x0
                values = (u0, x0, u1, xx0, u2, x * u1, x * (xx0 + u2), x * (x * u1) + u3)
                for k in range(8):
                    parts[k].append(values[k])
            target = 0 if sign else row_count - 1
            sums = tuple(
                old + jnp.where(rows_of == target, jnp.sum(sum(p), axis=0, keepdims=True), 0.0)
                for old, p in zip(sums, parts)
            )
        return sums

    def transport(c, sums):
        def body(shift, j, sums):
            iy = c * span + j
            iyg = iy0 + iy
            sy = speed_y(iyg)
            cy = jnp.full((row_count, cols), STEP * jnp.abs(sy), f32)

            rest = 1.0 - cy

            def moved(ix):
                sign, k = ix // HX, ix % HX
                lo = row_count * sign
                cur = pad[iy, sign, k, pl.ds(lo, row_count), :]
                near = pad[iy, sign, k, pl.ds(lo - 1 if sign else lo + 1, row_count), :]
                along = pltpu.roll(cur, shift, 1)
                cx = STEP * abs(speed_x(ix))
                new = cur * (rest - cx) + cx * near + cy * along
                conv[iy * VX + ix] = new
                return new

            s0 = s1 = s2 = s3 = jnp.zeros((row_count, cols), f32)
            for k in range(HX):
                low, high = moved(k), moved(VX - 1 - k)
                sx = speed_x(VX - 1 - k)
                even, odd = high + low, sx * (high - low)
                s0 = s0 + even
                s1 = s1 + odd
                s2 = s2 + (sx * sx) * even
                s3 = s3 + (sx * sx) * odd
            vy = jnp.full((row_count, cols), sy, f32)
            y2 = vy * vy
            a, b, cc, d, e, f, g, h = sums
            ys0 = vy * s0
            return (
                a + s0,
                b + s1,
                cc + ys0,
                d + s2,
                e + y2 * s0,
                f + vy * s1,
                g + s3 + y2 * s1,
                h + vy * s2 + y2 * ys0,
            )

        half = span // 2
        below = jnp.clip(lax.div(VY // 2 - iy0 - c * span, 2), 0, half)

        def pair(shift, j, sums):
            return body(shift, 2 * j + 1, body(shift, 2 * j, sums))

        sums = lax.fori_loop(0, below, functools.partial(pair, cols - 1), sums)
        return lax.fori_loop(below, half, functools.partial(pair, 1), sums)

    def copy_out(c):
        return pltpu.make_async_copy(
            conv.at[pl.ds(c * span * VX, span * VX)],
            conv_out.at[pl.ds(c * span * VX, span * VX)],
            out_sem.at[c],
        )

    def reduce_copy(it, r):
        return pltpu.make_async_remote_copy(
            src_ref=part.at[it, r],
            dst_ref=gath.at[it, me],
            send_sem=rs_send.at[it, r],
            recv_sem=rs_recv.at[it, me],
            device_id={"vel": first_owner + r, "space": here},
            device_id_type=MESH,
        )

    def row_copy(it, p, other):
        low = mine < SWEEPS
        target = jnp.where(low, left, right)
        slot = jnp.where(low, mine + SWEEPS + row_count, mine - (row_count - SWEEPS))
        if not other:
            target, slot = here, mine + SWEEPS
        return pltpu.make_async_remote_copy(
            src_ref=row_send.at[it],
            dst_ref=rows.at[it, slot],
            send_sem=ag_send.at[it, other, p],
            recv_sem=ag_recv.at[it, slot],
            device_id={"vel": p, "space": target},
            device_id_type=MESH,
        )

    def reduce(it, sums):
        for k in range(8):
            part[it, :, k, :] = sums[k] * QUAD
        for r in range(row_count):

            @pl.when(me != first_owner + r)
            def _():
                reduce_copy(it, r).start()

        @pl.when(owner)
        def _():
            gath[it, me] = part[it, mine]

            def add(i, sums):
                @pl.when(i != me)
                def _():
                    pltpu.make_async_remote_copy(
                        src_ref=part.at[it, 0],
                        dst_ref=gath.at[it, i],
                        send_sem=rs_send.at[it, 0],
                        recv_sem=rs_recv.at[it, i],
                        device_id={"vel": i, "space": here},
                        device_id_type=MESH,
                    ).wait_recv()

                sz = speed_z(velocity_base(i, vel_count)[1])
                value = gath[it, i]
                v1 = sz * value
                v2 = sz * v1
                v3 = sz * v2
                return (sums[0] + value, sums[1] + v1, sums[2] + v2, sums[3] + v3)

            zero = jnp.zeros((8, cols), f32)
            total = lax.fori_loop(0, groups, add, (zero, zero, zero, zero), unroll=min(16, groups))
            values = heat_row(*total)
            for k in range(8):
                row_send[it, pl.ds(k, 1), :] = values[k]
            rows[it, mine + SWEEPS] = row_send[it]

            def spread(p, carry):
                @pl.when(p != me)
                def _():
                    row_copy(it, p, 0).start()

                row_copy(it, p, 1).start()
                return carry

            lax.fori_loop(0, groups, spread, 0, unroll=4)

    def await_rows(it):
        for slot in range(row_count + 2 * SWEEPS):

            def wait():
                pltpu.make_async_remote_copy(
                    src_ref=row_send.at[it],
                    dst_ref=rows.at[it, slot],
                    send_sem=ag_send.at[it, 0, 0],
                    recv_sem=ag_recv.at[it, slot],
                    device_id={"vel": me, "space": right},
                    device_id_type=MESH,
                ).wait_recv()

            if SWEEPS <= slot < SWEEPS + row_count:
                pl.when(me != first_owner + slot - SWEEPS)(wait)
            else:
                wait()

    zero = jnp.zeros((row_count, cols), f32)
    zero8 = jnp.zeros((8, cols), f32)
    ready = nch - 1
    for it in range(ITERS):
        sums = (zero,) * 8
        if it == 0:
            for c in range(nch):
                if c <= ready:
                    arrived = range(c, nch) if c == ready else (c,)
                    for d in arrived:
                        for sign in range(2):
                            load_in(d, sign).wait()
                        pack_halo(it, d)
                if c == ready:
                    pl.semaphore_wait(barrier, 3 * groups - 1)
                    for d in range(nch):
                        send_halo(it, d)
                sums = transport(c, sums)
        else:
            await_rows(it - 1)
            diffuse_rows(rows.at[it - 1], tr, row_count)
            keep = macro_tables(tr, rate_ref, wall_ref, tab_x, tab_y, iy0, iz, iy_count)

            def load(iy, ix):
                return conv[iy * VX + ix]

            def store(iy, ix, value):
                sign, k = ix // HX, ix % HX
                pad[iy, sign, k, pl.ds(row_count * sign, row_count), :] = value

            for c in range(nch):
                collide(load, store, tab_x, tab_y, keep, c * span, span)
                pack_halo(it, c)
                send_halo(it, c)
                sums = transport(c, sums)
        added = ((zero8,) * 4,) * len(groups_x)
        for c in range(nch):
            added = fix_halo(it, c, added)
            if it == ITERS - 1:
                copy_out(c).start()
        reduce(it, add_fix(sums, added))
    last = ITERS - 1
    await_rows(last)
    rows_copy = pltpu.make_async_copy(rows.at[last], rows_out, out_sem.at[nch])
    rows_copy.start()
    for it in range(ITERS):
        for c in range(nch):
            for sign in range(2):
                halo(it, c, sign).wait_send()
        for r in range(row_count):

            @pl.when(me != first_owner + r)
            def _():
                reduce_copy(it, r).wait_send()

        @pl.when(owner)
        def _():
            def drain(p, carry):
                @pl.when(p != me)
                def _():
                    row_copy(it, p, 0).wait_send()

                row_copy(it, p, 1).wait_send()
                return carry

            lax.fori_loop(0, groups, drain, 0)

    for c in range(nch):
        copy_out(c).wait()
    rows_copy.wait()


def final_kernel(
    conv_in, rows, rate_ref, wall_ref, out, fields, buf, tr, tab_x, tab_y, in_sem, out_sem
):
    vel_count, row_count, cols = conv_in.shape
    iy_count = vel_count // VX
    nch = chunks_of(iy_count)
    span = iy_count // nch
    iy0, iz = velocity_base(lax.axis_index("vel"), vel_count)

    def piece(c):
        return pl.ds(c * span * VX, span * VX)

    def load_in(c):
        return pltpu.make_async_copy(conv_in.at[piece(c)], buf.at[piece(c)], in_sem.at[c])

    def copy_out(c):
        return pltpu.make_async_copy(buf.at[piece(c)], out.at[piece(c)], out_sem.at[c])

    for c in range(nch):
        load_in(c).start()
    diffuse_rows(rows, tr, row_count)
    for k in range(5):
        fields[k] = tr[:, k, :]
    keep = macro_tables(tr, rate_ref, wall_ref, tab_x, tab_y, iy0, iz, iy_count)

    def load(iy, ix):
        return buf[iy * VX + ix]

    def store(iy, ix, value):
        buf[iy * VX + ix] = value

    for c in range(nch):
        load_in(c).wait()
        collide(load, store, tab_x, tab_y, keep, c * span, span)
        copy_out(c).start()
    for c in range(nch):
        copy_out(c).wait()


def per_device(groups, tiles, distribution, rate_class, boundary_obstacle_indicator):
    vel_count, row_count, cols = distribution.shape
    iy_count = vel_count // VX
    nch = chunks_of(iy_count)
    vmem = pl.BlockSpec(memory_space=pltpu.VMEM)
    anywhere = pl.BlockSpec(memory_space=pl.ANY)
    total = row_count + 2 * SWEEPS
    tile = (row_count, cols)
    dma = pltpu.SemaphoreType.DMA
    conv, rows = pl.pallas_call(
        functools.partial(advance_kernel, groups, tiles),
        out_shape=(
            jax.ShapeDtypeStruct(distribution.shape, f32),
            jax.ShapeDtypeStruct((total, 8, cols), f32),
        ),
        in_specs=[anywhere, vmem, vmem],
        out_specs=(anywhere, anywhere),
        scratch_shapes=[
            pltpu.VMEM((iy_count, 2, HX, 2 * row_count, cols), f32),
            pltpu.VMEM((vel_count,) + tile, f32),
            pltpu.VMEM((ITERS, 2, iy_count, HX, cols), f32),
            pltpu.VMEM((ITERS, 2, iy_count, HX, cols), f32),
            pltpu.VMEM((ITERS, row_count, 8, cols), f32),
            pltpu.VMEM((ITERS, groups, 8, cols), f32),
            pltpu.VMEM((ITERS, 8, cols), f32),
            pltpu.VMEM((ITERS, total, 8, cols), f32),
            pltpu.VMEM((row_count, 8, cols), f32),
            pltpu.VMEM((3, VX) + tile, f32),
            pltpu.VMEM((3, iy_count) + tile, f32),
            dma((nch, 2)),
            dma((nch + 1,)),
            dma((ITERS, 2, nch)),
            dma((ITERS, 2, nch)),
            dma((ITERS, row_count)),
            dma((ITERS, groups)),
            dma((ITERS, 2, groups)),
            dma((ITERS, total)),
        ],
        compiler_params=pltpu.CompilerParams(collective_id=0, has_side_effects=True),
    )(
        distribution.reshape(iy_count, 2, HX, row_count, cols),
        rate_class,
        boundary_obstacle_indicator,
    )
    field, fields = pl.pallas_call(
        final_kernel,
        out_shape=(
            jax.ShapeDtypeStruct(distribution.shape, f32),
            jax.ShapeDtypeStruct((5,) + tile, f32),
        ),
        in_specs=[anywhere, vmem, vmem, vmem],
        out_specs=(anywhere, vmem),
        scratch_shapes=[
            pltpu.VMEM((vel_count,) + tile, f32),
            pltpu.VMEM((row_count, 8, cols), f32),
            pltpu.VMEM((3, VX) + tile, f32),
            pltpu.VMEM((3, iy_count) + tile, f32),
            dma((nch,)),
            dma((nch,)),
        ],
    )(conv, rows, rate_class, boundary_obstacle_indicator)
    return field, fields


def solution(mesh):
    placed = (P("vel", "space", None), P("space", None), P("space", None))
    return jax.shard_map(
        functools.partial(per_device, mesh.shape["vel"], mesh.shape["space"]),
        mesh=mesh,
        in_specs=placed,
        out_specs=(P("vel", "space", None), P(None, "space", None)),
        check_vma=False,
    )
```
